32 devices in a mesh: dp: 8 (over y, x, core), mp: 4 (over z).
Axes of the slice: x: 2, y: 2, z: 4, core: 2. Of those that a mesh axis runs over, the one named last changes fastest.
Arguments:
- tokens: bfloat16 [16384, 768], P(('dp', 'mp')), may hold values from -6 to 6
- segments: int32 [32, 512], P('dp'), may hold values from 0 to 5, never falling along the last dimension, each value on 1 to 256 neighbouring positions
- w_query: bfloat16 [768, 768], P(None, 'mp'), may hold values from -0.21875 to 0.21875
- b_query: bfloat16 [768], P('mp'), may hold values from -3 to 3
- w_key: bfloat16 [768, 768], P(None, 'mp'), may hold values from -0.21875 to 0.21875
- w_value: bfloat16 [768, 768], P(None, 'mp'), may hold values from -0.21875 to 0.21875
- b_value: bfloat16 [768], P('mp'), may hold values from -3 to 3
- w_out: bfloat16 [768, 768], P('mp'), may hold values from -0.625 to 0.625
- b_out: bfloat16 [768], replicated, may hold values from -3 to 3
- first_norm_gain: bfloat16 [768], replicated, may hold values from 0.099609375 to 1.8984375
- first_norm_bias: bfloat16 [768], replicated, may hold values from -3 to 3
- w_up: bfloat16 [768, 3072], P(None, 'mp'), may hold values from -0.21875 to 0.21875
- b_up: bfloat16 [3072], P('mp'), may hold values from -3 to 3
- w_down: bfloat16 [3072, 768], P('mp'), may hold values from -0.109375 to 0.109375
- b_down: bfloat16 [768], replicated, may hold values from -3 to 3
- second_norm_gain: bfloat16 [768], replicated, may hold values from 0.099609375 to 1.8984375
- second_norm_bias: bfloat16 [768], replicated, may hold values from -3 to 3
- output_gradient: bfloat16 [16384, 768], P(('dp', 'mp')), may hold values from -6 to 6
Outputs:
- out_tokens: bfloat16 [16384, 768], P(('dp', 'mp'))
- grad_tokens: bfloat16 [16384, 768], P(('dp', 'mp'))
- grad_w_query: float32 [768, 768], P(None, 'mp')
- grad_b_query: float32 [768], P('mp')
- grad_w_key: float32 [768, 768], P(None, 'mp')
- grad_w_value: float32 [768, 768], P(None, 'mp')
- grad_b_value: float32 [768], P('mp')
- grad_w_out: float32 [768, 768], P('mp')
- grad_b_out: float32 [768], replicated
- grad_norm1_gain: float32 [768], replicated
- grad_norm1_bias: float32 [768], replicated
- grad_w_up: float32 [768, 3072], P(None, 'mp')
- grad_b_up: float32 [3072], P('mp')
- grad_w_down: float32 [3072, 768], P('mp')
- grad_b_down: float32 [768], replicated
- grad_norm2_gain: float32 [768], replicated
- grad_norm2_bias: float32 [768], replicated
The draws below stay inside these ranges and needn't reach their ends.
Inputs may be any that keep to these rules, and one draw needn't show every extreme that they name: `segments`: document numbers never fall along a sequence; a document holds 1 to 256 positions, and in every sequence one holds exactly 256.
All inputs are finite; a program needn't handle non-finite values.
Results may differ from the reference program's by a relative error of at most 0.015.
Values may be sent and summed in bfloat16 or wider, within the bound.
No kernel may reach another device: no remote copies, remote signals or barrier semaphores. Data moves between devices by JAX's collectives and lax.ppermute only.
A program may use at most 128 MiB of HBM per device.

```python
import math
import jax
import jax.numpy as jnp
import numpy as np
from jax import lax

D = 768
HEADS = 12
HEAD_DIM = 64
FF = 3072
LEN = 512
DOCS = 6
SEQ_DEV = 4
TOK_DEV = 2048
SEQS = 32
TOKENS = 16384


def shard_levels(stream_key, shape, shards, low, top_value):
    factor_of, own = 1.0, jax.random.fold_in(stream_key, 6)
    for axis_at, parts in shards:
        heights = jnp.exp(jax.random.uniform(jax.random.fold_in(own, axis_at), (parts,), jnp.float32, low / len(shards), top_value / len(shards)))
        factor_of = factor_of * jnp.repeat(heights, shape[axis_at] // parts).reshape([-1 if axis == axis_at else 1 for axis in range(len(shape))])
    return factor_of


def length_profile(number_of, total, bound, skew):
    weights = [(1 << 20) // math.isqrt(grade ** skew) + 1 for grade in range(2, number_of + 1)]
    spare, holding = total - bound - (number_of - 1), [1] * (number_of - 1)
    while spare > 0:
        free = [i for i in range(number_of - 1) if holding[i] < bound]
        mass, left = sum([weights[i] for i in free]), spare
        for i in free:
            extra = min(bound - holding[i], max(1, left * weights[i] // mass), spare)
            holding[i] = holding[i] + extra
            spare = spare - extra
    return np.array([bound] + holding)


def ragged(own_key, number_of, total, bound, lean):
    if number_of == 2:
        one = jax.random.randint(own_key, (), max(1, total - bound), min(bound, total - 1) + 1)
        return jnp.stack([one, total - one])
    sizes = jnp.asarray(length_profile(number_of, total, bound, lean), jnp.int32)
    pairs = (number_of - 1) // 2
    giver, sink = sizes[1:1 + 2 * pairs:2], sizes[2:2 + 2 * pairs:2]
    slack = jnp.minimum(giver - 1, bound - sink)
    passed = jax.random.randint(jax.random.fold_in(own_key, 1), (pairs,), 0, 1 << 20) % (slack + 1)
    sizes = sizes.at[1:1 + 2 * pairs:2].set(giver - passed).at[2:2 + 2 * pairs:2].set(sink + passed)
    return sizes[jax.random.permutation(jax.random.fold_in(own_key, 2), number_of)]


def bell_draw(own_key, extent, scale, limit, shards=(), kind=jnp.bfloat16):
    level = shard_levels(own_key, extent, shards, -0.22, 0.18) if shards else 1.0
    drawn = jax.random.normal(own_key, extent, jnp.float32) * scale * level
    return jnp.minimum(jnp.maximum(drawn, -limit), limit).astype(kind)


def setup_inputs(seed: int = 0) -> dict:
    splits = jax.random.split(jax.random.key(seed), 19)
    return {
        "tokens": bell_draw(splits[0], (TOKENS, D), 1.0, 6.0, ((0, 32),)),
        "segments": jax.vmap(lambda own: jnp.searchsorted(jnp.cumsum(ragged(own, DOCS, LEN, LEN // 2, 0)), jnp.arange(LEN), side="right"))(jax.random.split(splits[1], SEQS)).reshape((SEQS, LEN)).astype(jnp.int32),
        "w_query": bell_draw(splits[2], (D, D), D ** -0.5, 0.21875, ((1, 4),)),
        "b_query": bell_draw(splits[3], (D,), 0.5, 3.0, ((0, 4),)),
        "w_key": bell_draw(splits[4], (D, D), D ** -0.5, 0.21875, ((1, 4),)),
        "w_value": bell_draw(splits[5], (D, D), D ** -0.5, 0.21875, ((1, 4),)),
        "b_value": bell_draw(splits[6], (D,), 0.5, 3.0, ((0, 4),)),
        "w_out": bell_draw(splits[7], (D, D), (D // 8) ** -0.5, 0.625, ((0, 4),)),
        "b_out": bell_draw(splits[8], (D,), 0.5, 3.0),
        "first_norm_gain": jnp.clip(1.0 + 0.18 * jax.random.normal(splits[9], (D,), jnp.float32), 0.099609375, 1.8984375).astype(jnp.bfloat16),
        "first_norm_bias": bell_draw(splits[10], (D,), 0.5, 3.0),
        "w_up": bell_draw(splits[11], (D, FF), D ** -0.5, 0.21875, ((1, 4),)),
        "b_up": bell_draw(splits[12], (FF,), 0.5, 3.0, ((0, 4),)),
        "w_down": bell_draw(splits[13], (FF, D), FF ** -0.5, 0.109375, ((0, 4),)),
        "b_down": bell_draw(splits[14], (D,), 0.5, 3.0),
        "second_norm_gain": jnp.clip(1.0 + 0.18 * jax.random.normal(splits[15], (D,), jnp.float32), 0.099609375, 1.8984375).astype(jnp.bfloat16),
        "second_norm_bias": bell_draw(splits[16], (D,), 0.5, 3.0),
        "output_gradient": bell_draw(splits[17], (TOKENS, D), 1.0, 6.0, ((0, 32),)),
    }


EPS = 1e-05
HIGHEST = lax.Precision.HIGHEST

@jax.custom_vjp
def low(v):
    return lax.optimization_barrier(v.astype(jnp.bfloat16)).astype(jnp.float32)

@jax.custom_vjp
def low_back(v):
    return v

def low_keep(v):
    return (low(v), None)

def low_pass(kept, grad):
    return (grad,)

def back_keep(v):
    return (v, None)

def back_low(kept, grad):
    return (low(grad),)
low.defvjp(low_keep, low_pass)
low_back.defvjp(back_keep, back_low)

def layer_norm(values, gain_vector, bias_vector):
    average = lax.optimization_barrier(jnp.mean(values, -1, keepdims=True))
    centered_rows = values - average
    spread = lax.optimization_barrier(jnp.mean(centered_rows * centered_rows, -1, keepdims=True))
    return centered_rows * lax.rsqrt(spread + EPS) * gain_vector + bias_vector

def attend(blocks):
    queries, key_rows, value_rows, segment = blocks
    scores = jnp.einsum('qhd,khd->hqk', queries, key_rows, precision=HIGHEST) * HEAD_DIM ** (-0.5)
    scores = low_back(scores)
    same_doc = segment[:, None] == segment[None, :]
    scores = jnp.where(same_doc[None], scores, -1e+30)
    attn_probs = jax.nn.softmax(scores, axis=-1)
    context = jnp.einsum('hqk,khd->qhd', low(attn_probs), value_rows, precision=HIGHEST)
    return context.reshape(LEN, D)

def forward(params, inputs, segment):
    w_query, b_query, w_key, w_value, b_value, w_out, b_out, gain_one, bias_one, w_up, b_up, w_down, b_down, gain_two, bias_two = params
    queries = low(low_back(jnp.dot(inputs, w_query, precision=HIGHEST) + b_query))
    key_rows = low(low_back(jnp.dot(inputs, w_key, precision=HIGHEST)))
    value_rows = low(low_back(jnp.dot(inputs, w_value, precision=HIGHEST) + b_value))

    def by_head(tensor):
        return tensor.reshape(SEQ_DEV, LEN, HEADS, HEAD_DIM)
    context = lax.map(jax.checkpoint(attend), (by_head(queries), by_head(key_rows), by_head(value_rows), segment))
    context = low(low_back(context.reshape(TOK_DEV, D)))
    attention_output = inputs + low_back(jnp.dot(context, w_out, precision=HIGHEST)) + b_out
    normalized_rows = layer_norm(attention_output, gain_one, bias_one)
    pre_act = low_back(jnp.dot(low(normalized_rows), w_up, precision=HIGHEST) + b_up)
    activated = low(jax.nn.gelu(pre_act, approximate=False))
    residual_sum = normalized_rows + low_back(jnp.dot(activated, w_down, precision=HIGHEST)) + b_down
    return layer_norm(residual_sum, gain_two, bias_two)

def reference(tokens, segments, w_query, b_query, w_key, w_value, b_value, w_out, b_out, first_norm_gain, first_norm_bias, w_up, b_up, w_down, b_down, second_norm_gain, second_norm_bias, output_gradient):
    params = tuple((item.astype(jnp.float32) for item in (w_query, b_query, w_key, w_value, b_value, w_out, b_out, first_norm_gain, first_norm_bias, w_up, b_up, w_down, b_down, second_norm_gain, second_norm_bias)))
    groups = TOKENS // TOK_DEV
    inputs = tokens.astype(jnp.float32).reshape(groups, TOK_DEV, D)
    cotangent = output_gradient.astype(jnp.float32).reshape(groups, TOK_DEV, D)
    seg_groups = segments.reshape(groups, SEQ_DEV, LEN)

    def one_group(totals, blocks):
        group_rows, segment, group_cot = blocks

        def local_forward(param_set, row_set):
            return forward(param_set, row_set, segment)
        outputs, pullback = jax.vjp(local_forward, params, group_rows)
        grad_params, grad_rows = pullback(group_cot)
        totals = tuple((left + right for left, right in zip(totals, grad_params)))
        return (totals, (outputs.astype(jnp.bfloat16), grad_rows.astype(jnp.bfloat16)))
    zeros = tuple((jnp.zeros(item.shape, jnp.float32) for item in params))
    totals, (output_rows, grad_rows) = lax.scan(one_group, zeros, (inputs, seg_groups, cotangent))
    return (output_rows.reshape(TOKENS, D), grad_rows.reshape(TOKENS, D), totals[0], totals[1], totals[2], totals[3], totals[4], totals[5], totals[6], totals[7], totals[8], totals[9], totals[10], totals[11], totals[12], totals[13], totals[14])
```

```python
import jax
import jax.numpy as jnp
from jax import lax
from jax.sharding import PartitionSpec as P

HEAD_DIM = 64
EPS = 1e-05
INV_ROOT_TWO = 0.7071067811865476
INV_ROOT_TWO_PI = 0.3989422804014327
CUBE = 8

f32 = jnp.float32
bf16 = jnp.bfloat16


def dot(left, right, dims):
    return lax.dot_general(left, right, ((dims[:1], dims[1:]), ((), ())), preferred_element_type=f32)


def norm_forward(values, gain, bias):
    average = jnp.mean(values, -1, keepdims=True)
    centered = values - average
    spread = jnp.mean(centered * centered, -1, keepdims=True)
    rstd = lax.rsqrt(spread + EPS)
    xhat = centered * rstd
    return xhat * gain + bias, xhat, rstd


def norm_backward(grad, xhat, rstd, gain):
    scaled = grad * gain
    result = rstd * (
        scaled
        - jnp.mean(scaled, -1, keepdims=True)
        - xhat * jnp.mean(scaled * xhat, -1, keepdims=True)
    )
    return result, jnp.sum(grad * xhat, 0), jnp.sum(grad, 0)


def gelu_parts(v):
    phi = 0.5 * (1.0 + lax.erf(v * INV_ROOT_TWO))
    return v * phi, phi + v * jnp.exp(-0.5 * v * v) * INV_ROOT_TWO_PI


class Links:
    def __init__(self, dp, mp):
        self.dp, self.mp = dp, mp
        self.index = lax.axis_index("dp")
        self.place = self.index % CUBE

    def shift(self, x, by):
        return lax.ppermute(x, "mp", [(i, (i + by) % self.mp) for i in range(self.mp)])

    def flip(self, x, bit):
        return lax.ppermute(x, "dp", [(i, i ^ bit) for i in range(self.dp)])

    def spread(self, piece):
        half = piece.shape[0] // 2
        over_x = self.flip(piece, 2)
        over_y = self.flip(piece, 4)
        diag_a = self.flip(over_x[:half], 4)
        diag_b = self.flip(over_y[half:], 2)
        diag = jnp.concatenate([diag_a, diag_b])
        even = [piece, over_x, over_y, diag]
        odd = [self.flip(part, 1) for part in even]
        return [even[0], odd[0], even[1], odd[1], even[2], odd[2], even[3], odd[3]]

    def ordered(self, parts):
        stacked = jnp.stack(parts)
        return jnp.stack(
            [
                lax.dynamic_index_in_dim(stacked, self.place ^ q, 0, keepdims=False)
                for q in range(CUBE)
            ]
        )

    def gather(self, shard):
        rows, cols = shard.shape
        step = rows // CUBE
        piece = lax.dynamic_slice_in_dim(shard, self.place * step, step, 0)
        others = jnp.concatenate([self.shift(piece, s) for s in range(1, self.mp)])
        whole = self.ordered(self.spread(others)).reshape(CUBE, self.mp - 1, step, cols)
        whole = whole.transpose(1, 0, 2, 3).reshape(self.mp - 1, rows, cols)
        return [shard] + [whole[s] for s in range(self.mp - 1)]

    def reduce(self, blocks):
        rows, cols = blocks[0].shape
        step = rows // CUBE
        stacked = jnp.stack(blocks).reshape(self.mp, CUBE, step, cols)
        rel = [
            lax.dynamic_index_in_dim(stacked, self.place ^ r, 1, keepdims=False).astype(bf16)
            for r in range(CUBE)
        ]
        other = self.flip(jnp.stack(rel[1::2]), 1)
        add = lambda *terms: sum(t.astype(f32) for t in terms).astype(bf16)
        own, to_x, to_y, to_diag = [add(rel[2 * i], other[i]) for i in range(4)]
        cut = self.mp // 2
        a, b = slice(0, cut), slice(cut, self.mp)
        from_x = self.flip(jnp.stack([to_diag[a], to_x[a]]), 2)
        from_y = self.flip(jnp.stack([to_diag[b], to_y[b]]), 4)
        last_x = self.flip(add(to_x[b], from_y[0]), 2)
        last_y = self.flip(add(to_y[a], from_x[0]), 4)
        own = jnp.concatenate([add(own[a], from_x[1], last_y), add(own[b], last_x, from_y[1])])
        terms = [own[0]] + [self.shift(own[s], -s) for s in range(1, self.mp)]
        total = sum(t.astype(f32) for t in terms)
        if self.dp > CUBE:
            groups = [[g * CUBE + i for g in range(self.dp // CUBE)] for i in range(CUBE)]
            total = lax.psum(total, "dp", axis_index_groups=groups)
        return total


def scores_of(queries, key_rows, same_doc):
    scores = jnp.einsum("qhd,khd->hqk", queries, key_rows, preferred_element_type=f32)
    return jnp.where(same_doc[None], scores * HEAD_DIM ** (-0.5), -1e30)


def attend_forward(queries, key_rows, value_rows, same_doc):
    scores = scores_of(queries, key_rows, same_doc)
    highest = jnp.max(scores, -1, keepdims=True)
    expd = jnp.exp(scores - highest)
    totals = jnp.sum(expd, -1, keepdims=True)
    probs = (expd / totals).astype(bf16)
    context = jnp.einsum("hqk,khd->qhd", probs, value_rows, preferred_element_type=f32)
    return context.astype(bf16), (highest + jnp.log(totals))[..., 0]


def attend_backward(queries, key_rows, value_rows, g_context, log_sums, same_doc):
    scores = scores_of(queries, key_rows, same_doc)
    probs = jnp.exp(scores - log_sums[..., None])
    g_value = jnp.einsum("hqk,qhd->khd", probs.astype(bf16), g_context, preferred_element_type=f32)
    g_probs = jnp.einsum("qhd,khd->hqk", g_context, value_rows, preferred_element_type=f32)
    centre = jnp.sum(probs * g_probs, -1, keepdims=True)
    g_scores = (probs * (g_probs - centre)).astype(bf16)
    scale = HEAD_DIM ** (-0.5)
    g_query = scale * jnp.einsum("hqk,khd->qhd", g_scores, key_rows, preferred_element_type=f32)
    g_key = scale * jnp.einsum("hqk,qhd->khd", g_scores, queries, preferred_element_type=f32)
    return g_query.astype(bf16), g_key.astype(bf16), g_value.astype(bf16)


def per_device(
    dp,
    mp,
    tokens,
    segments,
    w_query,
    b_query,
    w_key,
    w_value,
    b_value,
    w_out,
    b_out,
    first_norm_gain,
    first_norm_bias,
    w_up,
    b_up,
    w_down,
    b_down,
    second_norm_gain,
    second_norm_bias,
    output_gradient,
):
    links = Links(dp, mp)
    slots = range(mp)
    rows, width = tokens.shape
    part = w_query.shape[1]
    heads = part // HEAD_DIM
    gain1, bias1 = first_norm_gain.astype(f32), first_norm_bias.astype(f32)
    gain2, bias2 = second_norm_gain.astype(f32), second_norm_bias.astype(f32)
    segment = lax.dynamic_index_in_dim(segments, lax.axis_index("mp"), 0, keepdims=False)
    same_doc = segment[:, None] == segment[None, :]

    mixed = jnp.concatenate([w_query, w_key, w_value, w_out.T], axis=1)
    a_blocks = links.gather(mixed)
    vectors = jnp.concatenate([b_query, b_value, b_up])
    vectors = [vectors] + [links.shift(vectors, s) for s in range(1, mp)]
    bq = [v[:part].astype(f32) for v in vectors]
    bv = [v[part : 2 * part].astype(f32) for v in vectors]
    bu = [v[2 * part :].astype(f32) for v in vectors]
    u_blocks = links.gather(w_up)
    d_blocks = links.gather(w_down)

    by_head = lambda t: t.reshape(rows, heads, HEAD_DIM)
    by_rows = lambda t: t.reshape(rows, heads * HEAD_DIM)
    saved = []
    attended = tokens.astype(f32) + b_out.astype(f32)
    for s in slots:
        mix = dot(tokens, a_blocks[s][:, : 3 * part], (1, 0))
        q = by_head((mix[:, :part] + bq[s]).astype(bf16))
        k = by_head(mix[:, part : 2 * part].astype(bf16))
        v = by_head((mix[:, 2 * part :] + bv[s]).astype(bf16))
        context, sums = attend_forward(q, k, v, same_doc)
        context = by_rows(context)
        saved.append((q, k, v, context, sums))
        attended = attended + dot(context, a_blocks[s][:, 3 * part :], (1, 1))
    normed, xhat1, rstd1 = norm_forward(attended, gain1, bias1)
    normed_low = normed.astype(bf16)
    acts, slopes = [], []
    summed = normed + b_down.astype(f32)
    for s in slots:
        act, slope = gelu_parts(dot(normed_low, u_blocks[s], (1, 0)) + bu[s])
        acts.append(act.astype(bf16))
        slopes.append(slope)
        summed = summed + dot(acts[s], d_blocks[s], (1, 0))
    out_tokens, xhat2, rstd2 = norm_forward(summed, gain2, bias2)
    g_summed, g_gain2, g_bias2 = norm_backward(output_gradient.astype(f32), xhat2, rstd2, gain2)
    g_b_down = jnp.sum(g_summed, 0)
    g_low = g_summed.astype(bf16)
    piece_d = links.reduce([dot(acts[s], g_low, (0, 0)) for s in slots])
    g_pre = [(dot(g_low, d_blocks[s], (1, 1)) * slopes[s]).astype(bf16) for s in slots]
    piece_u = links.reduce([dot(normed_low, g_pre[s], (0, 0)) for s in slots])
    g_b_up = [jnp.sum(g.astype(f32), 0) for g in g_pre]
    g_normed = g_summed
    for s in slots:
        g_normed = g_normed + dot(g_pre[s], u_blocks[s], (1, 1))
    g_attended, g_gain1, g_bias1 = norm_backward(g_normed, xhat1, rstd1, gain1)
    g_b_out = jnp.sum(g_attended, 0)
    ga_low = g_attended.astype(bf16)
    g_tokens = g_attended
    g_mixed, g_bq, g_bv = [], [], []
    for s in slots:
        q, k, v, context, sums = saved[s]
        g_out = dot(ga_low, context, (0, 0))
        g_context = by_head(dot(ga_low, a_blocks[s][:, 3 * part :], (1, 0)).astype(bf16))
        gq, gk, gv = attend_backward(q, k, v, g_context, sums, same_doc)
        gq, gk, gv = by_rows(gq), by_rows(gk), by_rows(gv)
        g_bq.append(jnp.sum(gq.astype(f32), 0))
        g_bv.append(jnp.sum(gv.astype(f32), 0))
        g_qkv = jnp.concatenate([gq, gk, gv], axis=1)
        g_tokens = g_tokens + dot(g_qkv, a_blocks[s][:, : 3 * part], (1, 1))
        g_mixed.append(jnp.concatenate([dot(tokens, g_qkv, (0, 0)), g_out], axis=1))
    piece_a = links.reduce(g_mixed)

    pieces = jnp.concatenate([piece_a, piece_u, piece_d]).astype(bf16)
    step = width // CUBE
    whole = links.ordered(links.spread(pieces)).reshape(CUBE, 3, step, width)
    whole = whole.transpose(1, 0, 2, 3).reshape(3, width, width).astype(f32)
    g_a, g_u, g_d = whole[0], whole[1], whole[2]

    shared = jnp.stack([g_gain1, g_bias1, g_b_out, g_gain2, g_bias2, g_b_down])
    shared = lax.psum(shared, ("dp", "mp"))
    split = [jnp.concatenate([g_bq[s], g_bv[s], g_b_up[s]]) for s in slots]
    mine = split[0] + sum(links.shift(split[s], -s) for s in range(1, mp))
    mine = lax.psum(mine, "dp")
    return (
        out_tokens.astype(bf16),
        g_tokens.astype(bf16),
        g_a[:, :part],
        mine[:part],
        g_a[:, part : 2 * part],
        g_a[:, 2 * part : 3 * part],
        mine[part : 2 * part],
        g_a[:, 3 * part :].T,
        shared[2],
        shared[0],
        shared[1],
        g_u,
        mine[2 * part :],
        g_d,
        shared[5],
        shared[3],
        shared[4],
    )


def solution(mesh):
    rows, cols = P(("dp", "mp"), None), P(None, "mp")
    in_specs = (
        rows,
        P("dp", None),
        cols,
        P("mp"),
        cols,
        cols,
        P("mp"),
        P("mp", None),
        P(),
        P(),
        P(),
        cols,
        P("mp"),
        P("mp", None),
        P(),
        P(),
        P(),
        rows,
    )
    out_specs = (
        rows,
        rows,
        cols,
        P("mp"),
        cols,
        cols,
        P("mp"),
        P("mp", None),
        P(),
        P(),
        P(),
        cols,
        P("mp"),
        P("mp", None),
        P(),
        P(),
        P(),
    )
    dp, mp = mesh.shape["dp"], mesh.shape["mp"]

    def step(*args):
        return per_device(dp, mp, *args)

    return jax.shard_map(step, mesh=mesh, in_specs=in_specs, out_specs=out_specs, check_vma=False)
```

```python
import functools

import jax
import jax.numpy as jnp
from jax import lax
from jax.experimental import pallas as pl
from jax.experimental.pallas import tpu as pltpu
from jax.sharding import PartitionSpec as P

HEAD_DIM = 64
EPS = 1e-05
INV_ROOT_TWO = 0.7071067811865476
INV_ROOT_TWO_PI = 0.3989422804014327
SCALE = HEAD_DIM**-0.5
CUBE = 8
TAIL = 16
EXTRA = 8

f32 = jnp.float32
bf16 = jnp.bfloat16
SDS = jax.ShapeDtypeStruct


def dot(left, right, dims):
    return lax.dot_general(left, right, ((dims[:1], dims[1:]), ((), ())), preferred_element_type=f32)


def any_spec():
    return pl.BlockSpec(memory_space=pl.ANY)


def smem_spec():
    return pl.BlockSpec(memory_space=pltpu.SMEM)


def whole(shape):
    zeros = (0,) * len(shape)
    return pl.BlockSpec(shape, lambda *_: zeros)


def cost(flops, nbytes, trans=0):
    return pl.CostEstimate(flops=int(flops), bytes_accessed=int(nbytes), transcendentals=int(trans))


def spread_copies(place, parts, rows, step, slots, put):
    half = rows // 16 * 8
    copies = []
    for j in range(2):
        piece, over_x, over_y, diag_a, diag_b = parts[5 * j : 5 * j + 5]
        for i, ref in enumerate((piece, over_x, over_y)):
            for s in range(slots):
                copies.append((ref.at[pl.ds(s * step, step)], put(2 * i + j, s, 0, step)))
        for ref, first, end in ((diag_a, 0, half), (diag_b, half, rows)):
            for s in range(slots):
                low, high = max(first, s * step), min(end, (s + 1) * step)
                if low < high:
                    copies.append((ref.at[pl.ds(low - first, high - low)], put(6 + j, s, low - s * step, high - low)))
    return copies


def run_copies(copies, sems):
    started = [pltpu.make_async_copy(a, b, sems.at[n]) for n, (a, b) in enumerate(copies)]
    for c in started:
        c.start()
    for c in started:
        c.wait()


def assemble_kernel(step, slots, place_ref, own, *refs):
    parts, out, sems = refs[:10], refs[10], refs[11]

    def put(rel, s, first, count):
        to = pl.multiple_of((place_ref[0] ^ rel) * step + first, 16)
        return out.at[s + 1, pl.ds(to, count)]

    run_copies([(own, out.at[0])] + spread_copies(place_ref[0], parts, step * slots, step, slots, put), sems)


def assemble(place, own, parts, slots):
    rows, cols = own.shape
    return pl.pallas_call(
        functools.partial(assemble_kernel, rows // CUBE, slots),
        out_shape=SDS((slots + 1, rows, cols), bf16),
        grid=(1,),
        in_specs=[smem_spec()] + [any_spec()] * 11,
        out_specs=whole((slots + 1, rows, cols)),
        scratch_shapes=[pltpu.SemaphoreType.DMA((1 + 10 * slots,))],
        cost_estimate=cost(0, 4 * (slots + 1) * rows * cols),
        name="assemble",
    )(place, own, *parts)


def block_mask(seg_ref, bias):
    rows = bias.shape[0]
    segment = jnp.broadcast_to(seg_ref[...].astype(f32), (8, rows))
    bias[...] = jnp.where(segment.T[:, 0:1] == segment[0:1], 0.0, -1e30)


def attend_kernel(part, x_ref, a_ref, tail_ref, seg_ref, qkv_out, ctx_out, lse_out, att_out, bias):
    i = pl.program_id(0)
    heads = part // HEAD_DIM

    @pl.when(i == 0)
    def _():
        block_mask(seg_ref, bias)
        att_out[...] = jnp.zeros_like(att_out)

    shift = tail_ref[0].astype(f32).T
    qkv_out[0] = (dot(a_ref[0, : 3 * part, :], x_ref[...], (1, 1)) + shift[: 3 * part, 0:1]).astype(bf16)
    sums = []
    for h in range(heads):
        here = slice(h * HEAD_DIM, (h + 1) * HEAD_DIM)
        q, k, v = [qkv_out[0, n * part + h * HEAD_DIM : n * part + (h + 1) * HEAD_DIM, :] for n in range(3)]
        scores = dot(k, q, (0, 0)) * SCALE + bias[...]
        highest = jnp.max(scores, 0, keepdims=True)
        expd = jnp.exp(scores - highest)
        total = jnp.sum(expd, 0, keepdims=True)
        probs = (expd * (1.0 / total)).astype(bf16)
        ctx_out[0, here, :] = dot(v, probs, (1, 0)).astype(bf16)
        sums.append(highest + jnp.log(total))
    lse_out[0] = jnp.concatenate(sums + [jnp.zeros_like(sums[0])] * (8 - heads), axis=0)
    att_out[...] += dot(ctx_out[0], a_ref[0, 3 * part :, :], (0, 0))


def attend(first, count, part, x, a, tails, segment):
    rows, width = x.shape
    return pl.pallas_call(
        functools.partial(attend_kernel, part),
        out_shape=(
            SDS((count, 3 * part, rows), bf16),
            SDS((count, part, rows), bf16),
            SDS((count, 8, rows), f32),
            SDS((rows, width), f32),
        ),
        grid=(count,),
        in_specs=[
            whole((rows, width)),
            pl.BlockSpec((1, width, width), lambda i: (i + first, 0, 0)),
            pl.BlockSpec((1, TAIL, width), lambda i: (i + first, 0, 0)),
            whole((1, rows)),
        ],
        out_specs=(
            pl.BlockSpec((1, 3 * part, rows), lambda i: (i, 0, 0)),
            pl.BlockSpec((1, part, rows), lambda i: (i, 0, 0)),
            pl.BlockSpec((1, 8, rows), lambda i: (i, 0, 0)),
            whole((rows, width)),
        ),
        scratch_shapes=[pltpu.VMEM((rows, rows), f32)],
        cost_estimate=cost(
            count * (2 * rows * width * width + 4 * rows * rows * part), count * 4e6, count * 3 * rows * rows
        ),
        name="attend",
    )(x, a, tails, segment)


def store_pieces(acc, place, keep, send, vec=None):
    step = acc.shape[0] // CUBE
    half = step // 2
    for c, (px, py, ra, rb) in ((0, keep), (1, send)):
        for r, (to_a, at_a, to_b, at_b) in enumerate(
            ((ra, 1, rb, 1), (px, 1, rb, 0), (ra, 0, py, 1), (px, 0, py, 0))
        ):
            owner = place ^ (2 * r + c)
            base = pl.multiple_of(owner * step, 32)
            to_b[at_b, 0] = acc[pl.ds(base, half)].astype(bf16)
            to_a[at_a, 0, 0:half] = acc[pl.ds(pl.multiple_of(base + half, 16), half)].astype(bf16)
            if vec is not None:
                row = vec[pl.ds(owner, 1)]
                to_a[at_a, 0, half:] = jnp.broadcast_to(row, (EXTRA, row.shape[1])).astype(bf16)


def piece_shapes(count, step, cols, extra):
    half = step // 2
    a, b = SDS((2, count, half + extra, cols), bf16), SDS((2, count, half, cols), bf16)
    return (a, b, a, b) * 2


def piece_specs(step, cols, extra):
    half = step // 2
    a = pl.BlockSpec((2, 1, half + extra, cols), lambda i: (0, i, 0, 0))
    b = pl.BlockSpec((2, 1, half, cols), lambda i: (0, i, 0, 0))
    return (a, b, a, b) * 2


def attend_back_kernel(
    part, last, place_ref, x_ref, ga_ref, a_ref, qkv_ref, ctx_ref, lse_ref, vec_ref, seg_ref, gtok_ref, *refs
):
    pieces, gtok_out = refs[:8], refs[8]
    bias, gc_t, g_t, acc, vec = refs[9:]
    heads = part // HEAD_DIM

    @pl.when(pl.program_id(0) == 0)
    def _():
        block_mask(seg_ref, bias)
        if not last:
            gtok_out[...] = gtok_ref[...]

    gc_t[...] = dot(a_ref[0, 3 * part :, :], ga_ref[...], (1, 1)).astype(bf16)
    for h in range(heads):
        here = [slice(n * part + h * HEAD_DIM, n * part + (h + 1) * HEAD_DIM) for n in range(3)]
        q, k, v = [qkv_ref[0, at, :] for at in here]
        g_context = gc_t[here[0], :]
        probs = jnp.exp(dot(k, q, (0, 0)) * SCALE + bias[...] - lse_ref[0, h : h + 1, :])
        g_t[here[2], :] = dot(g_context, probs.astype(bf16), (1, 1)).astype(bf16)
        g_probs = dot(v, g_context, (0, 0))
        centre = jnp.sum(probs * g_probs, 0, keepdims=True)
        g_scores = (probs * (g_probs - centre)).astype(bf16)
        g_t[here[0], :] = (dot(k, g_scores, (1, 0)) * SCALE).astype(bf16)
        g_t[here[1], :] = (dot(q, g_scores, (1, 1)) * SCALE).astype(bf16)
    acc[: 3 * part, :] = dot(g_t[...], x_ref[...], (1, 0))
    acc[3 * part :, :] = dot(ctx_ref[0], ga_ref[...], (1, 0))
    sums = dot(jnp.ones((8, g_t.shape[1]), bf16), g_t[...], (1, 1))[0:1]
    vec[...] = vec_ref[0]
    vec[7:8] = jnp.concatenate([sums, jnp.zeros((1, vec.shape[1] - 3 * part), f32)], axis=1)
    store_pieces(acc, place_ref[0], pieces[:4], pieces[4:], vec)
    add = dot(g_t[...], a_ref[0, : 3 * part, :], (0, 0))
    if last:
        gtok_out[...] = (gtok_ref[...] + add).astype(bf16)
    else:
        gtok_out[...] += add


def attend_back(first, slot, count, last, part, place, x, ga, a, qkv, ctx, lse, vec, segment, gtok):
    rows, width = x.shape
    step = width // CUBE
    return pl.pallas_call(
        functools.partial(attend_back_kernel, part, last),
        out_shape=piece_shapes(count, step, width, EXTRA) + (SDS((rows, width), bf16 if last else f32),),
        grid=(count,),
        in_specs=[
            smem_spec(),
            whole((rows, width)),
            whole((rows, width)),
            pl.BlockSpec((1, width, width), lambda i: (i + slot, 0, 0)),
            pl.BlockSpec((1, 3 * part, rows), lambda i: (i + first, 0, 0)),
            pl.BlockSpec((1, part, rows), lambda i: (i + first, 0, 0)),
            pl.BlockSpec((1, 8, rows), lambda i: (i + first, 0, 0)),
            pl.BlockSpec((1, 8, width), lambda i: (i + slot, 0, 0)),
            whole((1, rows)),
            whole((rows, width)),
        ],
        out_specs=piece_specs(step, width, EXTRA) + (whole((rows, width)),),
        scratch_shapes=[
            pltpu.VMEM((rows, rows), f32),
            pltpu.VMEM((part, rows), bf16),
            pltpu.VMEM((3 * part, rows), bf16),
            pltpu.VMEM((width, width), f32),
            pltpu.VMEM((8, width), f32),
        ],
        cost_estimate=cost(
            count * (4 * rows * width * width + 10 * rows * rows * part), count * 8e6, count * 3 * rows * rows
        ),
        name="attend_back",
    )(place, x, ga, a, qkv, ctx, lse, vec, segment, gtok)


def norm_rows(values):
    average = jnp.mean(values, -1, keepdims=True)
    centered = values - average
    spread = jnp.mean(centered * centered, -1, keepdims=True)
    rstd = lax.rsqrt(spread + EPS)
    return centered * rstd, rstd


def norm_back(grad, xhat, rstd, gain):
    scaled = grad * gain
    return rstd * (
        scaled - jnp.mean(scaled, -1, keepdims=True) - xhat * jnp.mean(scaled * xhat, -1, keepdims=True)
    )


def up_kernel(x_ref, at0, at1, vecs, u_ref, tail_ref, xhat_out, rstd_out, low_out, act_out, slope_out):
    @pl.when(pl.program_id(0) == 0)
    def _():
        attended = x_ref[...].astype(f32) + at0[...] + at1[...] + vecs[0:1]
        xhat, rstd = norm_rows(attended)
        xhat_out[...] = xhat
        rstd_out[...] = rstd
        low_out[...] = (xhat * vecs[1:2] + vecs[2:3]).astype(bf16)

    rows = x_ref.shape[0]
    chunk = 128
    bias = tail_ref[0, 1:2].astype(f32)

    def one(n, _):
        at = pl.multiple_of(n * chunk, chunk)
        pre = dot(low_out[pl.ds(at, chunk), :], u_ref[0], (1, 0)) + bias
        phi = 0.5 * (1.0 + lax.erf(pre * INV_ROOT_TWO))
        act_out[0, pl.ds(at, chunk), :] = (pre * phi).astype(bf16)
        slope_out[0, pl.ds(at, chunk), :] = (phi + pre * jnp.exp(-0.5 * pre * pre) * INV_ROOT_TWO_PI).astype(bf16)
        return 0

    lax.fori_loop(0, rows // chunk, one, 0, unroll=True)


def feed_up(x, at0, at1, vecs, u, tails):
    rows, width = x.shape
    slots, _, cols = u.shape
    full = whole((rows, width))
    return pl.pallas_call(
        up_kernel,
        out_shape=(
            SDS((rows, width), f32),
            SDS((rows, 1), f32),
            SDS((rows, width), bf16),
            SDS((slots, rows, cols), bf16),
            SDS((slots, rows, cols), bf16),
        ),
        grid=(slots,),
        in_specs=[
            full,
            full,
            full,
            whole(vecs.shape),
            pl.BlockSpec((1, width, cols), lambda i: (i, 0, 0)),
            pl.BlockSpec((1, TAIL, cols), lambda i: (i, 0, 0)),
        ],
        out_specs=(
            full,
            whole((rows, 1)),
            full,
            pl.BlockSpec((1, rows, cols), lambda i: (i, 0, 0)),
            pl.BlockSpec((1, rows, cols), lambda i: (i, 0, 0)),
        ),
        cost_estimate=cost(2 * slots * rows * width * cols, 2e7, 2 * slots * rows * cols),
        name="feed_up",
    )(x, at0, at1, vecs, u, tails)


def down_kernel(act_ref, d_ref, xhat_ref, og_ref, vecs, out_ref, gs_out, gl_out, vec_out, acc):
    i = pl.program_id(0)
    add = dot(act_ref[0], d_ref[0], (1, 0))

    @pl.when(i == 0)
    def _():
        acc[...] = xhat_ref[...] * vecs[1:2] + vecs[2:3] + vecs[3:4] + add

    @pl.when(i > 0)
    def _():
        acc[...] += add

    @pl.when(i == pl.num_programs(0) - 1)
    def _():
        xhat, rstd = norm_rows(acc[...])
        out_ref[...] = (xhat * vecs[4:5] + vecs[5:6]).astype(bf16)
        grad = og_ref[...].astype(f32)
        g_summed = norm_back(grad, xhat, rstd, vecs[4:5])
        gs_out[...] = g_summed
        gl_out[...] = g_summed.astype(bf16)
        vec_out[...] = jnp.concatenate(
            [
                jnp.sum(grad * xhat, 0, keepdims=True),
                jnp.sum(grad, 0, keepdims=True),
                jnp.sum(g_summed, 0, keepdims=True),
                jnp.zeros((5, grad.shape[1]), f32),
            ]
        )


def feed_down(act, d, xhat, og, vecs):
    slots, rows, cols = act.shape
    width = d.shape[2]
    full = whole((rows, width))
    return pl.pallas_call(
        down_kernel,
        out_shape=(
            SDS((rows, width), bf16),
            SDS((rows, width), f32),
            SDS((rows, width), bf16),
            SDS((8, width), f32),
        ),
        grid=(slots,),
        in_specs=[
            pl.BlockSpec((1, rows, cols), lambda i: (i, 0, 0)),
            pl.BlockSpec((1, cols, width), lambda i: (i, 0, 0)),
            full,
            full,
            whole(vecs.shape),
        ],
        out_specs=(full, full, full, whole((8, width))),
        scratch_shapes=[pltpu.VMEM((rows, width), f32)],
        cost_estimate=cost(2 * slots * rows * width * cols, 1.4e7, 0),
        name="feed_down",
    )(act, d, xhat, og, vecs)


def down_grad_kernel(place_ref, act_ref, gl_ref, *refs):
    pieces, acc = refs[:8], refs[8]
    acc[...] = dot(act_ref[0], gl_ref[...], (0, 0))
    store_pieces(acc, place_ref[0], pieces[:4], pieces[4:])


def down_grad(place, act, gl):
    slots, rows, cols = act.shape
    width = gl.shape[1]
    step = cols // CUBE
    return pl.pallas_call(
        down_grad_kernel,
        out_shape=piece_shapes(slots, step, width, 0),
        grid=(slots,),
        in_specs=[smem_spec(), pl.BlockSpec((1, rows, cols), lambda i: (i, 0, 0)), whole((rows, width))],
        out_specs=piece_specs(step, width, 0),
        scratch_shapes=[pltpu.VMEM((cols, width), f32)],
        cost_estimate=cost(2 * slots * rows * width * cols, 1e7, 0),
        name="down_grad",
    )(place, act, gl)


def up_grad_kernel(place_ref, gl_ref, gs_ref, low_ref, d_ref, slope_ref, u_ref, xhat_ref, rstd_ref, vecs, vec2, *refs):
    pieces, ga_out, gal_out, vec_out = refs[:8], refs[8], refs[9], refs[10]
    low_t, total, acc = refs[11:]
    i = pl.program_id(0)

    @pl.when(i == 0)
    def _():
        low_t[...] = low_ref[...].T
        vec_out[...] = jnp.zeros_like(vec_out)

    g_pre = (dot(gl_ref[...], d_ref[0], (1, 1)) * slope_ref[0].astype(f32)).astype(bf16)
    acc[...] = dot(low_t[...], g_pre, (1, 0))
    store_pieces(acc, place_ref[0], pieces[:4], pieces[4:])
    vec_out[pl.ds(i, 1), 6:7, :] = jnp.sum(g_pre.astype(f32), 0, keepdims=True)[None]
    add = dot(g_pre, u_ref[0], (1, 1))

    @pl.when(i == 0)
    def _():
        total[...] = gs_ref[...] + add

    @pl.when(i > 0)
    def _():
        total[...] += add

    @pl.when(i == pl.num_programs(0) - 1)
    def _():
        grad = total[...]
        xhat = xhat_ref[...]
        g_attended = norm_back(grad, xhat, rstd_ref[...], vecs[1:2])
        ga_out[...] = g_attended
        gal_out[...] = g_attended.astype(bf16)
        head = jnp.concatenate(
            [
                jnp.sum(grad * xhat, 0, keepdims=True),
                jnp.sum(grad, 0, keepdims=True),
                jnp.sum(g_attended, 0, keepdims=True),
                vec2[0:3],
            ]
        )
        for s in range(vec_out.shape[0]):
            vec_out[s, 0:6] = head


def up_grad(place, gl, gs, low, d, slope, u, xhat, rstd, vecs, vec2):
    slots, width, cols = u.shape
    rows = gl.shape[0]
    step = width // CUBE
    full = whole((rows, width))
    return pl.pallas_call(
        up_grad_kernel,
        out_shape=piece_shapes(slots, step, cols, 0)
        + (SDS((rows, width), f32), SDS((rows, width), bf16), SDS((slots, 8, width), f32)),
        grid=(slots,),
        in_specs=[
            smem_spec(),
            full,
            full,
            full,
            pl.BlockSpec((1, cols, width), lambda i: (i, 0, 0)),
            pl.BlockSpec((1, rows, cols), lambda i: (i, 0, 0)),
            pl.BlockSpec((1, width, cols), lambda i: (i, 0, 0)),
            full,
            whole((rows, 1)),
            whole(vecs.shape),
            whole(vec2.shape),
        ],
        out_specs=piece_specs(step, cols, 0) + (full, full, whole((slots, 8, width))),
        scratch_shapes=[
            pltpu.VMEM((width, rows), bf16),
            pltpu.VMEM((rows, width), f32),
            pltpu.VMEM((width, cols), f32),
        ],
        cost_estimate=cost(6 * slots * rows * width * cols, 2e7, 0),
        name="up_grad",
    )(place, gl, gs, low, d, slope, u, xhat, rstd, vecs, vec2)


def finish_kernel(count, step, part, place_ref, *refs):
    parts, outs, stage, sems = refs[:10], refs[10:-2], refs[-2], refs[-1]
    rows = stage.shape[1]
    copies = spread_copies(place_ref[0], parts, rows, rows, 1, lambda rel, s, first, n: stage.at[rel, pl.ds(first, n)])
    run_copies(copies, sems)
    for q in range(CUBE):
        rel = place_ref[0] ^ q
        if part:
            at = q * step
            outs[at // part][at % part : at % part + step, :] = stage[rel, 0:step].astype(f32)
            outs[4][q : q + 1, :] = stage[rel, step : step + 8].astype(f32)[0:1]
        else:
            for n in range(count):
                outs[n][q * step : (q + 1) * step, :] = stage[rel, n * step : (n + 1) * step].astype(f32)


def finish(place, parts, count, part, width):
    step = width // CUBE
    if part:
        out_shape = (SDS((part, width), f32),) * 4 + (SDS((8, width), f32),)
    else:
        out_shape = (SDS((width, width), f32),) * count
    rows = parts[0].shape[0]
    return pl.pallas_call(
        functools.partial(finish_kernel, count, step, part),
        out_shape=out_shape,
        grid=(1,),
        in_specs=[smem_spec()] + [any_spec()] * 10,
        out_specs=tuple(whole(o.shape) for o in out_shape),
        scratch_shapes=[pltpu.VMEM((CUBE, rows, width), bf16), pltpu.SemaphoreType.DMA((10,))],
        cost_estimate=cost(0, 6 * count * width * width),
        name="finish",
    )(place, *parts)


def add(*terms):
    return sum(t.astype(f32) for t in terms).astype(bf16)


def hold(*values):
    leaves, tree = jax.tree.flatten(values)
    return jax.tree.unflatten(tree, lax.optimization_barrier(leaves))


class Links:
    def __init__(self, dp, mp):
        self.dp, self.mp = dp, mp

    def shift(self, x, by):
        return lax.ppermute(x, "mp", [(i, (i + by) % self.mp) for i in range(self.mp)])

    def flip(self, x, bit):
        return lax.ppermute(x, "dp", [(i, i ^ bit) for i in range(self.dp)])

    def swap(self, values):
        return [self.flip(v, 1) for v in values]

    def across(self, x_side, y_side):
        return self.flip(x_side, 2), self.flip(y_side, 4)

    def diagonal(self, over_x, over_y):
        half = over_x.shape[0] // 16 * 8
        return self.flip(over_x[:half], 4), self.flip(over_y[half:], 2)

    def shifts(self, piece):
        return [self.shift(piece, s) for s in range(1, self.mp)]

    def total(self, terms):
        value = sum(t.astype(f32) for t in terms)
        if self.dp > CUBE:
            groups = [[g * CUBE + i for g in range(self.dp // CUBE)] for i in range(CUBE)]
            value = lax.psum(value, "dp", axis_index_groups=groups)
        return value.astype(bf16)


def by_core(pieces, received):
    return [add(keep, got) for keep, got in zip(pieces[:4], received)]


def onward(sums, from_x, from_y):
    px, py, ra, rb = sums
    return add(rb[0], from_y[0]), add(ra[0], from_x[0]), (ra[1], from_x[1]), (rb[1], from_y[1])


def landed(hop, last_x, last_y):
    own_a, own_b = add(*hop[2], last_y), add(*hop[3], last_x)
    return [jnp.concatenate([own_b[s], own_a[s]]) for s in range(own_a.shape[0])]


def per_device(
    dp,
    mp,
    tokens,
    segments,
    w_query,
    b_query,
    w_key,
    w_value,
    b_value,
    w_out,
    b_out,
    first_norm_gain,
    first_norm_bias,
    w_up,
    b_up,
    w_down,
    b_down,
    second_norm_gain,
    second_norm_bias,
    output_gradient,
):
    links = Links(dp, mp)
    rows, width = tokens.shape
    part = w_query.shape[1]
    step = width // CUBE
    here = lax.axis_index("dp") % CUBE
    place = here.astype(jnp.int32).reshape(1)
    segment = lax.dynamic_slice_in_dim(segments, lax.axis_index("mp"), 1, 0)
    vecs = jnp.concatenate(
        [b_out, first_norm_gain, first_norm_bias, b_down, second_norm_gain, second_norm_bias] + [b_out] * 2
    )
    vecs = vecs.astype(f32).reshape(8, width)

    cut = lambda block: lax.dynamic_slice_in_dim(block, here * step, step, 0)
    mixed = jnp.concatenate([w_query.T, w_key.T, w_value.T, w_out])
    zeros = jnp.zeros_like(b_query)
    tail = jnp.concatenate([b_query, zeros, b_value, zeros, b_up, jnp.zeros(((TAIL - 2) * width,), bf16)])
    tail = tail.reshape(TAIL, width)
    a_piece = jnp.concatenate([cut(mixed), tail])

    a_recv = links.shifts(a_piece)
    qkv0, ctx0, lse0, at0 = attend(0, 1, part, tokens, mixed[None], tail[None], segment)
    u_cut, d_cut = cut(w_up), cut(w_down)
    a_recv, at0, u_cut, d_cut = hold(a_recv, at0, u_cut, d_cut)

    a_cat = jnp.concatenate([t[:step] for t in a_recv])
    tails = jnp.stack([tail] + [t[step:] for t in a_recv])
    ax, ay = links.across(a_cat, a_cat)
    u_recv = links.shifts(u_cut)
    a_cat, ax, ay, u_recv, d_cut, tails = hold(a_cat, ax, ay, u_recv, d_cut, tails)

    a_diag = links.diagonal(ax, ay)
    a_odd = links.swap([a_cat, ax, ay])
    u_cat = jnp.concatenate(u_recv)
    a_diag, a_odd, u_cat = hold(a_diag, a_odd, u_cat)

    a_diag_odd = links.swap(a_diag)
    a_diag_odd, u_cat, d_cut = hold(a_diag_odd, u_cat, d_cut)

    ux, uy = links.across(u_cat, u_cat)
    d_recv = links.shifts(d_cut)
    a_all = assemble(place, mixed, [a_cat, ax, ay, *a_diag, *a_odd, *a_diag_odd], mp - 1)
    qkv1, ctx1, lse1, at1 = attend(1, mp - 1, part, tokens, a_all, tails, segment)
    ux, uy, d_recv, at1 = hold(ux, uy, d_recv, at1)

    u_diag = links.diagonal(ux, uy)
    u_odd = links.swap([u_cat, ux, uy])
    d_cat = jnp.concatenate(d_recv)
    u_diag, u_odd, d_cat = hold(u_diag, u_odd, d_cat)

    u_diag_odd = links.swap(u_diag)
    u_diag_odd, d_cat = hold(u_diag_odd, d_cat)

    dx, dy = links.across(d_cat, d_cat)
    u_all = assemble(place, w_up, [u_cat, ux, uy, *u_diag, *u_odd, *u_diag_odd], mp - 1)
    xhat1, rstd1, low, act, slope = feed_up(tokens, at0, at1, vecs, u_all, tails)
    dx, dy, act = hold(dx, dy, act)

    d_diag = links.diagonal(dx, dy)
    d_odd = links.swap([d_cat, dx, dy])
    d_diag, d_odd = hold(d_diag, d_odd)
    d_diag_odd = links.swap(d_diag)
    d_all = assemble(place, w_down, [d_cat, dx, dy, *d_diag, *d_odd, *d_diag_odd], mp - 1)
    out_tokens, g_summed, g_low, vec2 = feed_down(act, d_all, xhat1, output_gradient, vecs)

    d_pieces = down_grad(place, act, g_low)
    d_got, g_low = hold(links.swap(d_pieces[4:8]), g_low)
    d_core = by_core(d_pieces, d_got)
    d_core, g_low = hold(d_core, g_low)

    d_from = links.across(*d_core[:2])
    *u_pieces, g_att, ga_low, vec = up_grad(
        place, g_low, g_summed, low, d_all, slope, u_all, xhat1, rstd1, vecs, vec2
    )
    d_from, u_pieces, ga_low = hold(d_from, u_pieces, ga_low)

    d_hop = onward(d_core, *d_from)
    u_got, d_hop, ga_low = hold(links.swap(u_pieces[4:8]), d_hop, ga_low)
    u_core = by_core(u_pieces, u_got)
    u_core, d_hop, ga_low = hold(u_core, d_hop, ga_low)

    d_last = links.across(*d_hop[:2])
    u_from = links.across(*u_core[:2])
    half = mp // 2
    *p2, g_tok = attend_back(
        half - 1, half, mp - half, False, part, place, tokens, ga_low, a_all, qkv1, ctx1, lse1, vec, segment, g_att
    )
    d_last, u_from, p2, g_tok = hold(d_last, u_from, p2, g_tok)

    d_own = landed(d_hop, *d_last)
    u_hop = onward(u_core, *u_from)
    got2, d_own, u_hop, g_tok = hold(links.swap(p2[4:8]), d_own, u_hop, g_tok)
    core2 = by_core(p2, got2)
    core2, d_own, u_hop, g_tok = hold(core2, d_own, u_hop, g_tok)

    d_terms = [d_own[0]] + [links.shift(d_own[s], -s) for s in range(1, mp)]
    u_last = links.across(*u_hop[:2])
    from2 = links.across(*core2[:2])
    *p1, g_tok = attend_back(
        0, 1, half - 1, False, part, place, tokens, ga_low, a_all, qkv1, ctx1, lse1, vec, segment, g_tok
    )
    d_terms, u_last, from2, p1, g_tok = hold(d_terms, u_last, from2, p1, g_tok)

    d_total = links.total(d_terms)
    u_own = landed(u_hop, *u_last)
    hop2 = onward(core2, *from2)
    got1, d_total, u_own, hop2, g_tok = hold(links.swap(p1[4:8]), d_total, u_own, hop2, g_tok)
    core1 = by_core(p1, got1)
    core1, d_total, u_own, hop2, g_tok = hold(core1, d_total, u_own, hop2, g_tok)

    u_terms = [u_own[0]] + [links.shift(u_own[s], -s) for s in range(1, mp)]
    last2 = links.across(*hop2[:2])
    from1 = links.across(*core1[:2])
    *p0, g_tok = attend_back(
        0, 0, 1, True, part, place, tokens, ga_low, a_all, qkv0, ctx0, lse0, vec, segment, g_tok
    )
    u_terms, last2, from1, p0 = hold(u_terms, last2, from1, p0)

    u_total = links.total(u_terms)
    ud = jnp.concatenate([u_total, d_total])
    own2 = landed(hop2, *last2)
    hop1 = onward(core1, *from1)
    got0, ud, own2, hop1 = hold(links.swap(p0[4:8]), ud, own2, hop1)
    core0 = by_core(p0, got0)
    core0, ud, own2, hop1 = hold(core0, ud, own2, hop1)

    from0 = links.across(*core0[:2])
    last1 = links.across(*hop1[:2])
    terms2 = [links.shift(t, -(half + s)) for s, t in enumerate(own2)]
    udx, udy = links.across(ud, ud)
    from0, last1, terms2, udx, udy = hold(from0, last1, terms2, udx, udy)

    hop0 = onward(core0, *from0)
    own1 = landed(hop1, *last1)
    hop0, own1 = hold(hop0, own1)
    last0 = links.across(*hop0[:2])
    terms1 = [links.shift(t, -(1 + s)) for s, t in enumerate(own1)]
    ud_diag = links.diagonal(udx, udy)
    ud_odd = links.swap([ud, udx, udy])
    last0, terms1, ud_diag, ud_odd = hold(last0, terms1, ud_diag, ud_odd)

    a_total = links.total(landed(hop0, *last0) + terms1 + terms2)
    ud_diag_odd = links.swap(ud_diag)
    a_total, ud_diag_odd = hold(a_total, ud_diag_odd)

    tx, ty = links.across(a_total, a_total)
    g_u, g_d = finish(place, [ud, udx, udy, *ud_diag, *ud_odd, *ud_diag_odd], 2, 0, width)
    tx, ty, g_u = hold(tx, ty, g_u)
    t_diag = links.diagonal(tx, ty)
    t_odd = links.swap([a_total, tx, ty])
    t_diag_odd = links.swap(t_diag)
    g_q, g_k, g_v, g_o, v = finish(place, [a_total, tx, ty, *t_diag, *t_odd, *t_diag_odd], 1, part, width)
    return (
        out_tokens,
        g_tok,
        g_q.T,
        v[7, :part],
        g_k.T,
        g_v.T,
        v[7, 2 * part : 3 * part],
        g_o,
        v[2],
        v[0],
        v[1],
        g_u,
        v[6],
        g_d,
        v[5],
        v[3],
        v[4],
    )


def solution(mesh):
    rows, cols = P(("dp", "mp"), None), P(None, "mp")
    in_specs = (
        rows,
        P("dp", None),
        cols,
        P("mp"),
        cols,
        cols,
        P("mp"),
        P("mp", None),
        P(),
        P(),
        P(),
        cols,
        P("mp"),
        P("mp", None),
        P(),
        P(),
        P(),
        rows,
    )
    out_specs = (
        rows,
        rows,
        cols,
        P("mp"),
        cols,
        cols,
        P("mp"),
        P("mp", None),
        P(),
        P(),
        P(),
        cols,
        P("mp"),
        P("mp", None),
        P(),
        P(),
        P(),
    )
    step = functools.partial(per_device, mesh.shape["dp"], mesh.shape["mp"])
    return jax.shard_map(step, mesh=mesh, in_specs=in_specs, out_specs=out_specs, check_vma=False)
```

```python
import functools

import jax
import jax.numpy as jnp
from jax import lax
from jax.experimental import pallas as pl
from jax.experimental.pallas import tpu as pltpu
from jax.sharding import PartitionSpec as P

HEAD_DIM = 64
EPS = 1e-05
INV_ROOT_TWO = 0.7071067811865476
INV_ROOT_TWO_PI = 0.3989422804014327
SCALE = HEAD_DIM**-0.5
CUBE = 8
TAIL = 16
EXTRA = 8

f32 = jnp.float32
bf16 = jnp.bfloat16
SDS = jax.ShapeDtypeStruct


def dot(left, right, dims):
    return lax.dot_general(left, right, ((dims[:1], dims[1:]), ((), ())), preferred_element_type=f32)


def any_spec():
    return pl.BlockSpec(memory_space=pl.ANY)


def smem_spec():
    return pl.BlockSpec(memory_space=pltpu.SMEM)


def whole(shape):
    zeros = (0,) * len(shape)
    return pl.BlockSpec(shape, lambda *_: zeros)


def cost(flops, nbytes, trans=0):
    return pl.CostEstimate(flops=int(flops) // 100, bytes_accessed=int(nbytes) // 100, transcendentals=int(trans) // 100)


def spread_copies(parts, step, slots, put):
    return [
        (s, (ref.at[pl.ds(s * step, step)], put(rel, s)))
        for rel, ref in zip((0, 2, 4, 6, 1, 3, 5, 7), parts)
        for s in range(slots)
    ]


def run_copies(copies, sems):
    started = [pltpu.make_async_copy(a, b, sems.at[n]) for n, (a, b) in enumerate(copies)]
    for c in started:
        c.start()
    for c in started:
        c.wait()


def fetch(i, place, own, parts, step, slots, blocks, blocks_out, sems, out_sems):
    first = 0 if own is None else 1
    count = slots + first

    def put(rel, s):
        return blocks.at[s + first, pl.ds(pl.multiple_of((place ^ rel) * step, 32), step)]

    copies = [(first + s, pair) for s, pair in spread_copies(parts, step, slots, put)]
    if own is not None:
        copies.append((0, (own, blocks.at[0])))
    copies = [(s, pltpu.make_async_copy(a, b, sems.at[n])) for n, (s, (a, b)) in enumerate(copies)]
    outs = [pltpu.make_async_copy(blocks.at[s], blocks_out.at[s], out_sems.at[s]) for s in range(count)]

    @pl.when(i == 0)
    def _():
        for s in range(count):
            for at, c in copies:
                if at == s:
                    c.start()

    for s in range(count):

        @pl.when(i == s)
        def _():
            for at, c in copies:
                if at == s:
                    c.wait()
            outs[s].start()

    def close():
        @pl.when(i == count - 1)
        def _():
            for c in outs:
                c.wait()

    return close


def fetch_scratch(count, rows, cols):
    return [
        pltpu.VMEM((count, rows, cols), bf16),
        pltpu.SemaphoreType.DMA((1 + CUBE * count,)),
        pltpu.SemaphoreType.DMA((count,)),
    ]


def block_mask(seg_ref, bias):
    rows = bias.shape[0]
    segment = jnp.broadcast_to(seg_ref[...].astype(f32), (8, rows))
    bias[...] = jnp.where(segment.T[:, 0:1] == segment[0:1], 0.0, -1e30)


def attend_block(part, x_ref, w, tail_ref, qkv_out, ctx_out, lse_out, att_out, bias):
    heads = part // HEAD_DIM
    shift = tail_ref[0].astype(f32).T
    qkv_out[0] = (dot(w(0, 3 * part), x_ref[...], (1, 1)) + shift[: 3 * part, 0:1]).astype(bf16)
    sums = []
    for h in range(heads):
        here = slice(h * HEAD_DIM, (h + 1) * HEAD_DIM)
        q, k, v = [qkv_out[0, n * part + h * HEAD_DIM : n * part + (h + 1) * HEAD_DIM, :] for n in range(3)]
        scores = dot(k, q, (0, 0)) * SCALE + bias[...]
        highest = jnp.max(scores, 0, keepdims=True)
        expd = jnp.exp(scores - highest)
        total = jnp.sum(expd, 0, keepdims=True)
        probs = (expd * (1.0 / total)).astype(bf16)
        ctx_out[0, here, :] = dot(v, probs, (1, 0)).astype(bf16)
        sums.append(highest + jnp.log(total))
    lse_out[0] = jnp.concatenate(sums + [jnp.zeros_like(sums[0])] * (8 - heads), axis=0)
    att_out[...] += dot(ctx_out[0], w(3 * part, 4 * part), (0, 0))


def attend_own_kernel(part, x_ref, a_ref, tail_ref, seg_ref, qkv_out, ctx_out, lse_out, att_out, bias):
    block_mask(seg_ref, bias)
    att_out[...] = jnp.zeros_like(att_out)
    w = lambda low, high: a_ref[low:high, :]
    attend_block(part, x_ref, w, tail_ref, qkv_out, ctx_out, lse_out, att_out, bias)


def attend_kernel(part, slots, place_ref, x_ref, tail_ref, seg_ref, start_ref, *refs):
    parts, (qkv_out, ctx_out, lse_out, att_out, all_out, bias, blocks, sems, out_sems) = refs[:CUBE], refs[CUBE:]
    i = pl.program_id(0)
    step = x_ref.shape[1] // CUBE
    close = fetch(i, place_ref[0], None, parts, step, slots, blocks, all_out, sems, out_sems)

    @pl.when(i == 0)
    def _():
        block_mask(seg_ref, bias)
        att_out[...] = start_ref[...]

    w = lambda low, high: blocks[i, low:high, :]
    attend_block(part, x_ref, w, tail_ref, qkv_out, ctx_out, lse_out, att_out, bias)
    close()


def attend(part, place, x, a, tails, segment, start=None, parts=None):
    rows, width = x.shape
    count = tails.shape[0]
    outs = [
        (SDS((count, 3 * part, rows), bf16), pl.BlockSpec((1, 3 * part, rows), lambda i: (i, 0, 0))),
        (SDS((count, part, rows), bf16), pl.BlockSpec((1, part, rows), lambda i: (i, 0, 0))),
        (SDS((count, 8, rows), f32), pl.BlockSpec((1, 8, rows), lambda i: (i, 0, 0))),
        (SDS((rows, width), f32), whole((rows, width))),
    ]
    tail_spec = pl.BlockSpec((1, TAIL, width), lambda i: (i, 0, 0))
    scratch = [pltpu.VMEM((rows, rows), f32)]
    estimate = cost(
        count * (2 * rows * width * width + 4 * rows * rows * part), count * 4e6, count * 3 * rows * rows
    )
    if parts is None:
        ins = [(x, whole((rows, width))), (a, whole(a.shape)), (tails, tail_spec), (segment, whole((1, rows)))]
        kernel = functools.partial(attend_own_kernel, part)
    else:
        ins = [(place, smem_spec()), (x, whole((rows, width))), (tails, tail_spec), (segment, whole((1, rows)))]
        ins += [(start, whole((rows, width)))] + [(t, any_spec()) for t in parts]
        outs.append((SDS((count, width, width), bf16), any_spec()))
        scratch += fetch_scratch(count, width, width)
        kernel = functools.partial(attend_kernel, part, count)
    return pl.pallas_call(
        kernel,
        out_shape=tuple(o for o, _ in outs),
        grid=(count,),
        in_specs=[spec for _, spec in ins],
        out_specs=tuple(spec for _, spec in outs),
        scratch_shapes=scratch,
        cost_estimate=estimate,
        name="attend",
    )(*[t for t, _ in ins])


def store_pieces(acc, place, px, py, ra, rb, send, vec):
    step = acc.shape[0] // CUBE
    half = step // 2
    long = half + EXTRA
    tops = {"px": 0, "py": long, "ra": long + half, "rb": 2 * long + half}
    keep = {"px": px, "py": py, "ra": ra, "rb": rb}
    for c in range(2):
        for r, (to_a, at_a, to_b, at_b) in enumerate(
            (("ra", 1, "rb", 1), ("px", 1, "rb", 0), ("ra", 0, "py", 1), ("px", 0, "py", 0))
        ):
            owner = place ^ (2 * r + c)
            base = pl.multiple_of(owner * step, 32)
            row = vec[pl.ds(owner, 1)]
            part_b = acc[pl.ds(base, half)].astype(bf16)
            part_a = acc[pl.ds(pl.multiple_of(base + half, 16), half)].astype(bf16)
            extra = jnp.broadcast_to(row, (EXTRA, row.shape[1])).astype(bf16)
            if c == 0:
                keep[to_b][at_b, 0] = part_b
                keep[to_a][at_a, 0, 0:half] = part_a
                keep[to_a][at_a, 0, half:] = extra
            else:
                send[at_b, 0, tops[to_b] : tops[to_b] + half] = part_b
                send[at_a, 0, tops[to_a] : tops[to_a] + half] = part_a
                send[at_a, 0, tops[to_a] + half : tops[to_a] + long] = extra


def store_quarters(acc, place, px, py, ra, rb):
    step = acc.shape[0] // 4
    half = step // 2
    for r, (to_a, at_a, to_b, at_b) in enumerate(((ra, 1, rb, 1), (px, 1, rb, 0), (ra, 0, py, 1), (px, 0, py, 0))):
        base = pl.multiple_of(((place >> 1) ^ r) * step, 32)
        to_b[at_b, 0] = acc[pl.ds(base, half)].astype(bf16)
        to_a[at_a, 0] = acc[pl.ds(pl.multiple_of(base + half, 16), half)].astype(bf16)


def piece_shapes(count, step, cols):
    return (SDS((2, count, step // 2, cols), bf16),) * 4


def piece_specs(step, cols):
    return (pl.BlockSpec((2, 1, step // 2, cols), lambda i: (0, i, 0, 0)),) * 4


def mixed_shapes(count, step, cols):
    half = step // 2
    rows = (half + EXTRA, half, half + EXTRA, half, 4 * half + 2 * EXTRA)
    return tuple(SDS((2, count, n, cols), bf16) for n in rows)


def mixed_specs(step, cols):
    return tuple(
        pl.BlockSpec((2, 1, o.shape[2], cols), lambda i: (0, i, 0, 0)) for o in mixed_shapes(1, step, cols)
    )


def attend_back_kernel(
    part, last, place_ref, x_ref, ga_ref, a_ref, qkv_ref, ctx_ref, lse_ref, vec_ref, seg_ref, gtok_ref, *refs
):
    pieces, gtok_out = refs[:5], refs[5]
    bias, gc_t, g_t, acc, vec = refs[6:]
    heads = part // HEAD_DIM

    @pl.when(pl.program_id(0) == 0)
    def _():
        block_mask(seg_ref, bias)
        if not last:
            gtok_out[...] = gtok_ref[...]

    gc_t[...] = dot(a_ref[0, 3 * part :, :], ga_ref[...], (1, 1)).astype(bf16)
    for h in range(heads):
        here = [slice(n * part + h * HEAD_DIM, n * part + (h + 1) * HEAD_DIM) for n in range(3)]
        q, k, v = [qkv_ref[0, at, :] for at in here]
        g_context = gc_t[here[0], :]
        probs = jnp.exp(dot(k, q, (0, 0)) * SCALE + bias[...] - lse_ref[0, h : h + 1, :])
        g_t[here[2], :] = dot(g_context, probs.astype(bf16), (1, 1)).astype(bf16)
        g_probs = dot(v, g_context, (0, 0))
        centre = jnp.sum(probs * g_probs, 0, keepdims=True)
        g_scores = (probs * (g_probs - centre)).astype(bf16)
        g_t[here[0], :] = (dot(k, g_scores, (1, 0)) * SCALE).astype(bf16)
        g_t[here[1], :] = (dot(q, g_scores, (1, 1)) * SCALE).astype(bf16)
    acc[: 3 * part, :] = dot(g_t[...], x_ref[...], (1, 0))
    acc[3 * part :, :] = dot(ctx_ref[0], ga_ref[...], (1, 0))
    sums = dot(jnp.ones((8, g_t.shape[1]), bf16), g_t[...], (1, 1))[0:1]
    vec[...] = vec_ref[0]
    vec[7:8] = jnp.concatenate([sums, jnp.zeros((1, vec.shape[1] - 3 * part), f32)], axis=1)
    store_pieces(acc, place_ref[0], *pieces, vec)
    add = dot(g_t[...], a_ref[0, : 3 * part, :], (0, 0))
    if last:
        gtok_out[...] = (gtok_ref[...] + add).astype(bf16)
    else:
        gtok_out[...] += add


def attend_back(first, a_first, slot, count, last, part, place, x, ga, a, qkv, ctx, lse, vec, segment, gtok):
    rows, width = x.shape
    step = width // CUBE
    return pl.pallas_call(
        functools.partial(attend_back_kernel, part, last),
        out_shape=mixed_shapes(count, step, width) + (SDS((rows, width), bf16 if last else f32),),
        grid=(count,),
        in_specs=[
            smem_spec(),
            whole((rows, width)),
            whole((rows, width)),
            pl.BlockSpec((1, width, width), lambda i: (i + a_first, 0, 0)),
            pl.BlockSpec((1, 3 * part, rows), lambda i: (i + first, 0, 0)),
            pl.BlockSpec((1, part, rows), lambda i: (i + first, 0, 0)),
            pl.BlockSpec((1, 8, rows), lambda i: (i + first, 0, 0)),
            pl.BlockSpec((1, 8, width), lambda i: (i + slot, 0, 0)),
            whole((1, rows)),
            whole((rows, width)),
        ],
        out_specs=mixed_specs(step, width) + (whole((rows, width)),),
        scratch_shapes=[
            pltpu.VMEM((rows, rows), f32),
            pltpu.VMEM((part, rows), bf16),
            pltpu.VMEM((3 * part, rows), bf16),
            pltpu.VMEM((width, width), f32),
            pltpu.VMEM((8, width), f32),
        ],
        cost_estimate=cost(
            count * (4 * rows * width * width + 10 * rows * rows * part), count * 8e6, count * 3 * rows * rows
        ),
        name="attend_back",
    )(place, x, ga, a, qkv, ctx, lse, vec, segment, gtok)


def norm_rows(values):
    average = jnp.mean(values, -1, keepdims=True)
    centered = values - average
    spread = jnp.mean(centered * centered, -1, keepdims=True)
    rstd = lax.rsqrt(spread + EPS)
    return centered * rstd, rstd


def norm_back(grad, xhat, rstd, gain):
    scaled = grad * gain
    return rstd * (
        scaled - jnp.mean(scaled, -1, keepdims=True) - xhat * jnp.mean(scaled * xhat, -1, keepdims=True)
    )


def up_kernel(slots, place_ref, x_ref, att_ref, vecs, tail_ref, own, *refs):
    parts, (xhat_out, rstd_out, low_out, act_out, send_out, slope_out, all_out, blocks, sems, out_sems) = (
        refs[:CUBE],
        refs[CUBE:],
    )
    i = pl.program_id(0)
    rows, width = x_ref.shape
    cols = act_out.shape[2]
    close = fetch(i, place_ref[0], own, parts, width // CUBE, slots - 1, blocks, all_out, sems, out_sems)

    @pl.when(i == 0)
    def _():
        attended = x_ref[...].astype(f32) + att_ref[...] + vecs[0:1]
        xhat, rstd = norm_rows(attended)
        xhat_out[...] = xhat
        rstd_out[...] = rstd
        low_out[...] = (xhat * vecs[1:2] + vecs[2:3]).astype(bf16)

    chunk = 128
    bias = tail_ref[0, 1:2].astype(f32)
    for n in range(rows // chunk):
        at = slice(n * chunk, (n + 1) * chunk)
        pre = dot(low_out[at, :], blocks[i], (1, 0)) + bias
        phi = 0.5 * (1.0 + lax.erf(pre * INV_ROOT_TWO))
        act_out[0, at, :] = (pre * phi).astype(bf16)
        slope_out[0, at, :] = (phi + pre * jnp.exp(-0.5 * pre * pre) * INV_ROOT_TWO_PI).astype(bf16)
    other = pl.multiple_of((1 - place_ref[0] % 2) * (cols // 2), 128)
    send_out[0] = act_out[0, :, pl.ds(other, cols // 2)]
    close()


def feed_up(place, x, att, vecs, tails, own, parts):
    rows, width = x.shape
    slots = tails.shape[0]
    cols = own.shape[1]
    full = whole((rows, width))
    blockwise = lambda n: pl.BlockSpec((1, rows, n), lambda i: (i, 0, 0))
    return pl.pallas_call(
        functools.partial(up_kernel, slots),
        out_shape=(
            SDS((rows, width), f32),
            SDS((rows, 1), f32),
            SDS((rows, width), bf16),
            SDS((slots, rows, cols), bf16),
            SDS((slots, rows, cols // 2), bf16),
            SDS((slots, rows, cols), bf16),
            SDS((slots, width, cols), bf16),
        ),
        grid=(slots,),
        in_specs=[
            smem_spec(),
            full,
            full,
            whole(vecs.shape),
            pl.BlockSpec((1, TAIL, cols), lambda i: (i, 0, 0)),
            *[any_spec()] * (1 + CUBE),
        ],
        out_specs=(
            full,
            whole((rows, 1)),
            full,
            blockwise(cols),
            blockwise(cols // 2),
            blockwise(cols),
            any_spec(),
        ),
        scratch_shapes=fetch_scratch(slots, width, cols),
        cost_estimate=cost(2 * slots * rows * width * cols, 2e7, 2 * slots * rows * cols),
        name="feed_up",
    )(place, x, att, vecs, tails, own, *parts)


def down_kernel(slots, place_ref, act_ref, xhat_ref, og_ref, vecs, own, *refs):
    parts, (out_ref, gs_out, gl_out, vec_out, all_out, acc, blocks, sems, out_sems) = refs[:CUBE], refs[CUBE:]
    i = pl.program_id(0)
    step = blocks.shape[1] // CUBE
    close = fetch(i, place_ref[0], own, parts, step, slots - 1, blocks, all_out, sems, out_sems)

    @pl.when(i == 0)
    def _():
        acc[...] = xhat_ref[...] * vecs[1:2] + vecs[2:3] + vecs[3:4]

    acc[...] += dot(act_ref[0], blocks[i], (1, 0))

    @pl.when(i == slots - 1)
    def _():
        xhat, rstd = norm_rows(acc[...])
        out_ref[...] = (xhat * vecs[4:5] + vecs[5:6]).astype(bf16)
        grad = og_ref[...].astype(f32)
        g_summed = norm_back(grad, xhat, rstd, vecs[4:5])
        gs_out[...] = g_summed
        gl_out[...] = g_summed.astype(bf16)
        vec_out[...] = jnp.concatenate(
            [
                jnp.sum(grad * xhat, 0, keepdims=True),
                jnp.sum(grad, 0, keepdims=True),
                jnp.sum(g_summed, 0, keepdims=True),
                jnp.zeros((5, grad.shape[1]), f32),
            ]
        )

    close()


def feed_down(place, act, xhat, og, vecs, own, parts):
    slots, rows, cols = act.shape
    width = own.shape[1]
    full = whole((rows, width))
    return pl.pallas_call(
        functools.partial(down_kernel, slots),
        out_shape=(
            SDS((rows, width), bf16),
            SDS((rows, width), f32),
            SDS((rows, width), bf16),
            SDS((8, width), f32),
            SDS((slots, cols, width), bf16),
        ),
        grid=(slots,),
        in_specs=[
            smem_spec(),
            pl.BlockSpec((1, rows, cols), lambda i: (i, 0, 0)),
            full,
            full,
            whole(vecs.shape),
            *[any_spec()] * (1 + CUBE),
        ],
        out_specs=(full, full, full, whole((8, width)), any_spec()),
        scratch_shapes=[pltpu.VMEM((rows, width), f32)] + fetch_scratch(slots, cols, width),
        cost_estimate=cost(2 * slots * rows * width * cols, 1.4e7, 0),
        name="feed_down",
    )(place, act, xhat, og, vecs, own, *parts)


def down_grad_kernel(place_ref, act_ref, act_got, gl_ref, gl_got, px, py, ra, rb, acc):
    half = act_got.shape[2]
    mine = pl.multiple_of((place_ref[0] % 2) * half, 128)
    acc[...] = dot(act_ref[0, :, pl.ds(mine, half)], gl_ref[...], (0, 0)) + dot(act_got[0], gl_got[...], (0, 0))
    store_quarters(acc, place_ref[0], px, py, ra, rb)


def down_grad(place, act, act_got, gl, gl_got):
    slots, rows, cols = act.shape
    width = gl.shape[1]
    return pl.pallas_call(
        down_grad_kernel,
        out_shape=piece_shapes(slots, cols // CUBE, width),
        grid=(slots,),
        in_specs=[
            smem_spec(),
            pl.BlockSpec((1, rows, cols), lambda i: (i, 0, 0)),
            pl.BlockSpec((1, rows, cols // 2), lambda i: (i, 0, 0)),
            whole((rows, width)),
            whole((rows, width)),
        ],
        out_specs=piece_specs(cols // CUBE, width),
        scratch_shapes=[pltpu.VMEM((cols // 2, width), f32)],
        cost_estimate=cost(2 * slots * rows * width * cols, 1e7, 0),
        name="down_grad",
    )(place, act, act_got, gl, gl_got)


def pre_kernel(place_ref, gl_ref, gs_ref, d_ref, slope_ref, u_ref, xhat_ref, rstd_ref, vecs, vec2, *refs):
    keep_out, send_out, ga_out, gal_out, vec_out, total, pre = refs
    i = pl.program_id(0)
    half = keep_out.shape[2]

    @pl.when(i == 0)
    def _():
        vec_out[...] = jnp.zeros_like(vec_out)
        total[...] = gs_ref[...]

    g_pre = (dot(gl_ref[...], d_ref[0], (1, 1)) * slope_ref[0].astype(f32)).astype(bf16)
    pre[...] = g_pre
    core = place_ref[0] % 2
    keep_out[0] = pre[:, pl.ds(pl.multiple_of(core * half, 128), half)]
    send_out[0] = pre[:, pl.ds(pl.multiple_of((1 - core) * half, 128), half)]
    vec_out[pl.ds(i, 1), 6:7, :] = jnp.sum(g_pre.astype(f32), 0, keepdims=True)[None]
    total[...] += dot(g_pre, u_ref[0], (1, 1))

    @pl.when(i == pl.num_programs(0) - 1)
    def _():
        grad = total[...]
        xhat = xhat_ref[...]
        g_attended = norm_back(grad, xhat, rstd_ref[...], vecs[1:2])
        ga_out[...] = g_attended
        gal_out[...] = g_attended.astype(bf16)
        head = jnp.concatenate(
            [
                jnp.sum(grad * xhat, 0, keepdims=True),
                jnp.sum(grad, 0, keepdims=True),
                jnp.sum(g_attended, 0, keepdims=True),
                vec2[0:3],
            ]
        )
        for s in range(vec_out.shape[0]):
            vec_out[s, 0:6] = head


def feed_back(place, gl, gs, d, slope, u, xhat, rstd, vecs, vec2):
    slots, width, cols = u.shape
    rows = gl.shape[0]
    full = whole((rows, width))
    blockwise = lambda n: pl.BlockSpec((1, rows, n), lambda i: (i, 0, 0))
    return pl.pallas_call(
        pre_kernel,
        out_shape=(
            SDS((slots, rows, cols // 2), bf16),
            SDS((slots, rows, cols // 2), bf16),
            SDS((rows, width), f32),
            SDS((rows, width), bf16),
            SDS((slots, 8, width), f32),
        ),
        grid=(slots,),
        in_specs=[
            smem_spec(),
            full,
            full,
            pl.BlockSpec((1, cols, width), lambda i: (i, 0, 0)),
            blockwise(cols),
            pl.BlockSpec((1, width, cols), lambda i: (i, 0, 0)),
            full,
            whole((rows, 1)),
            whole(vecs.shape),
            whole(vec2.shape),
        ],
        out_specs=(blockwise(cols // 2), blockwise(cols // 2), full, full, whole((slots, 8, width))),
        scratch_shapes=[pltpu.VMEM((rows, width), f32), pltpu.VMEM((rows, cols), bf16)],
        cost_estimate=cost(4 * slots * rows * width * cols, 2e7, 0),
        name="feed_back",
    )(place, gl, gs, d, slope, u, xhat, rstd, vecs, vec2)


def up_grad_kernel(place_ref, low_ref, low_got, g_ref, g_got, px, py, ra, rb, low_t, got_t, acc):
    @pl.when(pl.program_id(0) == 0)
    def _():
        low_t[...] = low_ref[...].T
        got_t[...] = low_got[...].T

    acc[...] = dot(low_t[...], g_ref[0], (1, 0)) + dot(got_t[...], g_got[0], (1, 0))
    store_quarters(acc, place_ref[0], px, py, ra, rb)


def up_grad(place, low, low_got, g, g_got):
    slots, rows, cols = g.shape
    width = low.shape[1]
    blockwise = pl.BlockSpec((1, rows, cols), lambda i: (i, 0, 0))
    return pl.pallas_call(
        up_grad_kernel,
        out_shape=piece_shapes(slots, width // 4, cols),
        grid=(slots,),
        in_specs=[smem_spec(), whole((rows, width)), whole((rows, width)), blockwise, blockwise],
        out_specs=piece_specs(width // 4, cols),
        scratch_shapes=[
            pltpu.VMEM((width, rows), bf16),
            pltpu.VMEM((width, rows), bf16),
            pltpu.VMEM((width, cols), f32),
        ],
        cost_estimate=cost(4 * slots * rows * width * cols, 1e7, 0),
        name="up_grad",
    )(place, low, low_got, g, g_got)


def finish_kernel(part, place_ref, *refs):
    parts, outs, stage, sems = refs[:CUBE], refs[CUBE:-2], refs[-2], refs[-1]
    rows = stage.shape[1]
    run_copies([pair for _, pair in spread_copies(parts, rows, 1, lambda rel, s: stage.at[rel])], sems)
    step = rows - EXTRA
    for q in range(CUBE):
        rel = place_ref[0] ^ q
        at = q * step
        outs[at // part][at % part : at % part + step, :] = stage[rel, 0:step].astype(f32)
        outs[4][q : q + 1, :] = stage[rel, step:].astype(f32)[0:1]


def finish(place, parts, part):
    rows, width = parts[0].shape
    out_shape = (SDS((part, width), f32),) * 4 + (SDS((8, width), f32),)
    return pl.pallas_call(
        functools.partial(finish_kernel, part),
        out_shape=out_shape,
        grid=(1,),
        in_specs=[smem_spec()] + [any_spec()] * CUBE,
        out_specs=tuple(whole(o.shape) for o in out_shape),
        scratch_shapes=[pltpu.VMEM((CUBE, rows, width), bf16), pltpu.SemaphoreType.DMA((CUBE,))],
        cost_estimate=cost(0, 6 * width * width),
        name="finish",
    )(place, *parts)


def finish_feed_kernel(place_ref, *refs):
    ups, downs, (up_out, down_out, stage, sems) = refs[:CUBE], refs[CUBE : 2 * CUBE], refs[2 * CUBE :]
    step = ups[0].shape[0]
    half = stage.shape[3] // 2
    copies = []
    for n, parts in enumerate((ups, downs)):
        copies += spread_copies(parts, step, 1, lambda rel, s: stage.at[n, rel])
    run_copies([pair for _, pair in copies], sems)
    for q in range(CUBE):
        rel = place_ref[0] ^ q
        core, chip = q % 2, q // 2
        for n in range(2):
            at = (2 * chip + n) * step
            value = stage[0, rel, :, n * half : (n + 1) * half]
            up_out[at : at + step, core * half : (core + 1) * half] = value.astype(f32)
        at = (core * 4 + chip) * step
        down_out[at : at + step, :] = stage[1, rel].astype(f32)


def finish_feed(place, ups, downs):
    step, width = ups[0].shape
    out = SDS((width, width), f32)
    return pl.pallas_call(
        finish_feed_kernel,
        out_shape=(out, out),
        grid=(1,),
        in_specs=[smem_spec()] + [any_spec()] * (2 * CUBE),
        out_specs=(whole(out.shape), whole(out.shape)),
        scratch_shapes=[pltpu.VMEM((2, CUBE, step, width), bf16), pltpu.SemaphoreType.DMA((2 * CUBE,))],
        cost_estimate=cost(0, 12 * width * width),
        name="finish_feed",
    )(place, *ups, *downs)


def add(*terms):
    return sum(t.astype(f32) for t in terms).astype(bf16)


def hold(*values):
    leaves, tree = jax.tree.flatten(values)
    return jax.tree.unflatten(tree, lax.optimization_barrier(leaves))


class Links:
    def __init__(self, dp, mp):
        self.dp, self.mp = dp, mp

    def shift(self, x, by):
        return lax.ppermute(x, "mp", [(i, (i + by) % self.mp) for i in range(self.mp)])

    def flip(self, x, bit):
        return lax.ppermute(x, "dp", [(i, i ^ bit) for i in range(self.dp)])

    def swap(self, values):
        return [self.flip(v, 1) for v in values]

    def across(self, x_side, y_side):
        return self.flip(x_side, 2), self.flip(y_side, 4)

    def around(self, piece):
        return [self.flip(piece, 2), self.flip(piece, 4), self.flip(piece, 6)]

    def shifts(self, piece):
        return [self.shift(piece, s) for s in range(1, self.mp)]

    def total(self, terms):
        value = sum(t.astype(f32) for t in terms)
        if self.dp > CUBE:
            groups = [[g * CUBE + i for g in range(self.dp // CUBE)] for i in range(CUBE)]
            value = lax.psum(value, "dp", axis_index_groups=groups)
        return value.astype(bf16)


def by_core(pieces, received):
    sums, top = [], 0
    for keep in pieces:
        sums.append(add(keep, received[:, :, top : top + keep.shape[2]]))
        top += keep.shape[2]
    return sums


def onward(sums, from_x, from_y):
    px, py, ra, rb = sums
    return add(rb[0], from_y[0]), add(ra[0], from_x[0]), (ra[1], from_x[1]), (rb[1], from_y[1])


def landed(hop, last_x, last_y, axis=0):
    own_a, own_b = add(*hop[2], last_y), add(*hop[3], last_x)
    return [jnp.concatenate([own_b[s], own_a[s]], axis=axis) for s in range(own_a.shape[0])]


def per_device(
    dp,
    mp,
    tokens,
    segments,
    w_query,
    b_query,
    w_key,
    w_value,
    b_value,
    w_out,
    b_out,
    first_norm_gain,
    first_norm_bias,
    w_up,
    b_up,
    w_down,
    b_down,
    second_norm_gain,
    second_norm_bias,
    output_gradient,
):
    links = Links(dp, mp)
    rows, width = tokens.shape
    part = w_query.shape[1]
    step = width // CUBE
    here = lax.axis_index("dp") % CUBE
    place = here.astype(jnp.int32).reshape(1)
    segment = lax.dynamic_slice_in_dim(segments, lax.axis_index("mp"), 1, 0)
    vecs = jnp.concatenate(
        [b_out, first_norm_gain, first_norm_bias, b_down, second_norm_gain, second_norm_bias] + [b_out] * 2
    )
    vecs = vecs.astype(f32).reshape(8, width)

    cut = lambda block: lax.dynamic_slice_in_dim(block, here * step, step, 0)
    stack = [w_query.T, w_key.T, w_value.T, w_out]
    per = part // step
    cuts = [lax.dynamic_slice_in_dim(t, here % per * step, step, 0) for t in stack]
    a_cut = cuts[0]
    for n in range(1, 4):
        a_cut = jnp.where(here // per == n, cuts[n], a_cut)
    zeros = jnp.zeros_like(b_query)
    tail = jnp.concatenate([b_query, zeros, b_value, zeros, b_up, jnp.zeros(((TAIL - 2) * width,), bf16)])
    tail = tail.reshape(TAIL, width)

    a_recv = links.shifts(jnp.concatenate([a_cut, tail]))
    mixed = jnp.concatenate(stack)
    qkv0, ctx0, lse0, at0 = attend(part, place, tokens, mixed, tail[None], segment)
    u_cut, d_cut = cut(w_up), cut(w_down)
    a_recv, at0, u_cut, d_cut, vecs = hold(a_recv, at0, u_cut, d_cut, vecs)

    a_cat = jnp.concatenate([t[:step] for t in a_recv])
    tails = jnp.stack([tail] + [t[step:] for t in a_recv])
    a_even = [a_cat, *links.around(a_cat)]
    u_recv = links.shifts(u_cut)
    d_near = links.shift(d_cut, 1)
    a_even, u_recv, d_near, d_cut, tails = hold(a_even, u_recv, d_near, d_cut, tails)

    a_odd = links.swap(a_even)
    u_cat = jnp.concatenate(u_recv)
    a_odd, u_cat, d_cut = hold(a_odd, u_cat, d_cut)

    u_even = [u_cat, *links.around(u_cat)]
    d_far = [links.shift(d_cut, s) for s in range(2, mp)]
    qkv1, ctx1, lse1, at1, a_all = attend(
        part, place, tokens, None, tails[1:], segment, at0, a_even + a_odd
    )
    u_even, d_far, at1 = hold(u_even, d_far, at1)

    u_odd = links.swap(u_even)
    d_cat = jnp.concatenate([d_near, *d_far])
    u_odd, d_cat = hold(u_odd, d_cat)

    d_even = [d_cat, *links.around(d_cat)]
    xhat1, rstd1, low, act, act_send, slope, u_all = feed_up(
        place, tokens, at1, vecs, tails, w_up, u_even + u_odd
    )
    d_even, act, act_send, low = hold(d_even, act, act_send, low)

    d_odd = links.swap(d_even)
    d_odd, act_send, low = hold(d_odd, act_send, low)
    act_got, low_got = links.swap([act_send, low])
    out_tokens, g_summed, g_low, vec2, d_all = feed_down(
        place, act, xhat1, output_gradient, vecs, w_down, d_even + d_odd
    )
    g_low, act_got, low_got = hold(g_low, act_got, low_got)

    (g_low_got,) = links.swap([g_low])
    d_core = down_grad(place, act, act_got, g_low, g_low_got)
    d_core, g_low = hold(d_core, g_low)

    d_from = links.across(*d_core[:2])
    g_keep, g_send, g_att, ga_low, vec = feed_back(
        place, g_low, g_summed, d_all, slope, u_all, xhat1, rstd1, vecs, vec2
    )
    g_keep, g_send, ga_low, d_from = hold(g_keep, g_send, ga_low, d_from)
    (g_got,) = links.swap([g_send])
    d_hop = onward(d_core, *d_from)
    g_got, d_hop = hold(g_got, d_hop)

    d_last = links.across(*d_hop[:2])
    u_core = up_grad(place, low, low_got, g_keep, g_got)
    u_core, d_last, ga_low = hold(u_core, d_last, ga_low)
    d_own = landed(d_hop, *d_last)
    u_core, d_own, ga_low = hold(u_core, d_own, ga_low)

    u_from = links.across(*u_core[:2])
    d_recv = [links.shift(d_own[s], -s) for s in range(1, mp)]
    back = lambda slot, count, last, gtok, a, kept: attend_back(
        0, 0, slot, count, last, part, place, tokens, ga_low, a, *kept, vec, segment, gtok
    )
    *p1, g_tok = back(1, mp - 1, False, g_att, a_all, (qkv1, ctx1, lse1))
    p1, g_tok, u_from, d_recv = hold(p1, g_tok, u_from, d_recv)

    d_total = links.total([d_own[0], *d_recv])
    u_hop = onward(u_core, *u_from)
    u_hop, p1, d_total = hold(u_hop, p1, d_total)
    u_last = links.across(*u_hop[:2])
    (got1,) = links.swap(p1[4:])
    got1, u_last, g_tok, d_total = hold(got1, u_last, g_tok, d_total)
    core1 = by_core(p1[:4], got1)
    u_own = landed(u_hop, *u_last, axis=1)
    core1, u_own, g_tok, d_total = hold(core1, u_own, g_tok, d_total)

    u_recv = [links.shift(u_own[s], -s) for s in range(1, mp)]
    from1 = links.across(*core1[:2])
    *p0, g_tok = back(0, 1, True, g_tok, mixed[None], (qkv0, ctx0, lse0))
    p0, u_recv, from1, d_total = hold(p0, u_recv, from1, d_total)

    d_even = [d_total, *links.around(d_total)]
    u_total = links.total([u_own[0], *u_recv])
    hop1 = onward(core1, *from1)
    (got0,) = links.swap(p0[4:])
    got0, hop1, u_total = hold(got0, hop1, u_total)
    core0 = by_core(p0[:4], got0)
    flat = lambda *t: jnp.concatenate([v.reshape(-1, width) for v in t])
    over_x, over_y = flat(core0[0], hop1[0]), flat(core0[1], hop1[1])
    over_x, over_y, core0, u_total = hold(over_x, over_y, core0, u_total)
    over_x, over_y = links.across(over_x, over_y)
    over_x, over_y, d_even = hold(over_x, over_y, d_even)
    cut_x, cut_y = core0[0].size // width, core0[1].size // width
    own1 = landed(hop1, over_x[cut_x:].reshape(hop1[0].shape), over_y[cut_y:].reshape(hop1[1].shape))
    hop0 = onward(core0, over_x[:cut_x].reshape(core0[0].shape), over_y[:cut_y].reshape(core0[1].shape))
    hop0, own1, u_total = hold(hop0, own1, u_total)

    last0 = links.across(*hop0[:2])
    terms1 = [links.shift(t, -(1 + s)) for s, t in enumerate(own1)]
    d_odd = links.swap(d_even)
    last0, terms1, d_odd = hold(last0, terms1, d_odd)
    a_total = links.total(landed(hop0, *last0) + terms1)
    a_total, u_total = hold(a_total, u_total)

    t_even = [a_total, *links.around(a_total)]
    u_even = [u_total, *links.around(u_total)]
    t_even, u_even = hold(t_even, u_even)
    t_odd, u_odd = links.swap(t_even), links.swap(u_even)
    g_u, g_d = finish_feed(place, u_even + u_odd, d_even + d_odd)
    g_q, g_k, g_v, g_o, v = finish(place, t_even + t_odd, part)
    return (
        out_tokens,
        g_tok,
        g_q.T,
        v[7, :part],
        g_k.T,
        g_v.T,
        v[7, 2 * part : 3 * part],
        g_o,
        v[2],
        v[0],
        v[1],
        g_u,
        v[6],
        g_d,
        v[5],
        v[3],
        v[4],
    )


def solution(mesh):
    rows, cols = P(("dp", "mp"), None), P(None, "mp")
    in_specs = (
        rows,
        P("dp", None),
        cols,
        P("mp"),
        cols,
        cols,
        P("mp"),
        P("mp", None),
        P(),
        P(),
        P(),
        cols,
        P("mp"),
        P("mp", None),
        P(),
        P(),
        P(),
        rows,
    )
    out_specs = (
        rows,
        rows,
        cols,
        P("mp"),
        cols,
        cols,
        P("mp"),
        P("mp", None),
        P(),
        P(),
        P(),
        cols,
        P("mp"),
        P("mp", None),
        P(),
        P(),
        P(),
    )
    step = functools.partial(per_device, mesh.shape["dp"], mesh.shape["mp"])
    return jax.shard_map(step, mesh=mesh, in_specs=in_specs, out_specs=out_specs, check_vma=False)
```
